512 devices in a mesh: seq: 128 (over x, z, core), head: 4 (over y).
Axes of the slice: x: 4, y: 4, z: 16, core: 2. Of those that a mesh axis runs over, the one named last changes fastest.
Arguments:
- query_states: bfloat16 [16384, 2048], P('seq', 'head'), may hold values from -24.5 to 24.5
- key_states: bfloat16 [16384, 512], P('seq', 'head'), may hold values from -10.5 to 10.5
- value_states: bfloat16 [16384, 512], P('seq', 'head'), may hold values from -6 to 6
- out_weight: bfloat16 [2048, 4096], P('head'), may hold values from -0.125 to 0.125
- block_docs: int32 [128], replicated, may hold values from 0 to 63, never falling along the last dimension, each value on 1 to 32 neighbouring positions
Outputs:
- mixed: bfloat16 [16384, 4096], P('seq', 'head')
The draws below stay inside these ranges and needn't reach their ends.
Inputs may be any that keep to these rules, and one draw needn't show every extreme that they name: `block_docs`: A document spans at most 32 blocks.
All inputs are finite; a program needn't handle non-finite values.
Results may differ from the reference program's by a relative error of at most 0.0095.
Values may be sent and summed in bfloat16 or wider, within the bound.
A program may use at most 64 MiB of HBM per device.

```python
import math
import jax
import jax.numpy as jnp
import numpy as np
from jax import lax

D = 4096
HD = 128
QH = 16
KH = 4
BLK = 128
TOK_DEV = 128
TOKENS = 16384
NBLK = 128
MOST = 32
DOCS = 64
N_SEQ = 128
N_HEAD = 4


def base_keys(key):
    return jnp.clip(jax.random.normal(jax.random.fold_in(key, 11), (TOKENS, KH * HD), jnp.float32), -3.5, 3.5)


def draw_key_states(key, part):
    base = base_keys(key)
    return base.astype(jnp.bfloat16)


def draw_query_states(key, part):
    drawn = jnp.clip(jax.random.normal(jax.random.fold_in(key, 12), (TOKENS, QH * HD), jnp.float32), -3.5, 3.5)
    return drawn.astype(jnp.bfloat16)


def block_scale(rng, shape, shards, low, largest):
    level = 1.0
    for axis_at, parts in shards:
        steps = jax.random.uniform(jax.random.fold_in(jax.random.fold_in(rng, 6), axis_at), (parts,), jnp.float32, low / len(shards), largest / len(shards))
        level = level * jnp.repeat(jnp.exp(steps), shape[axis_at] // parts).reshape((-1,) + (1,) * (len(shape) - 1 - axis_at))
    return level


def length_profile(count, total, limit, skew):
    portions = [(1 << 20) // math.isqrt(rank ** skew) + 1 for rank in range(2, count + 1)]
    surplus, holding = total - limit - (count - 1), [1] * (count - 1)
    while surplus > 0:
        movable = [i for i in range(count - 1) if holding[i] < limit]
        mass, remaining = sum([portions[i] for i in movable]), surplus
        for i in movable:
            addition = min(limit - holding[i], max(1, remaining * portions[i] // mass), surplus)
            holding[i] = holding[i] + addition
            surplus = surplus - addition
    return np.array([limit] + holding)


def ragged_sizes(own_key, amount, total, limit, slope):
    if amount == 2:
        one = jax.random.randint(own_key, (), max(1, total - limit), min(limit, total - 1) + 1)
        return jnp.stack([one, total - one])
    lengths = jnp.asarray(length_profile(amount, total, limit, slope), jnp.int32)
    couples = (amount - 1) // 2
    source_of, sink = lengths[1:1 + 2 * couples:2], lengths[2:2 + 2 * couples:2]
    margin = jnp.minimum(source_of - 1, limit - sink)
    shifted = jax.random.randint(jax.random.fold_in(own_key, 1), (couples,), 0, 1 << 20) % (margin + 1)
    lengths = lengths.at[1:1 + 2 * couples:2].set(source_of - shifted).at[2:2 + 2 * couples:2].set(sink + shifted)
    return lengths[jax.random.permutation(jax.random.fold_in(own_key, 2), amount)]


def noise(key, extent, spread, reach, shards=(), kind=jnp.bfloat16):
    drawn = spread * jax.random.normal(key, extent, jnp.float32)
    if shards:
        drawn = drawn * block_scale(key, extent, shards, -0.22, 0.18)
    return jnp.clip(drawn, -reach, reach).astype(kind)


def setup_inputs(seed: int = 0) -> dict:
    streams_of = jax.random.split(jax.random.key(seed), 6)
    query_states = draw_query_states(jax.random.fold_in(streams_of[5], 71), 0)
    key_states = draw_key_states(jax.random.fold_in(streams_of[5], 71), 0)
    value_states = noise(streams_of[2], (TOKENS, KH * HD), 1.0, 6.0, ((0, 128), (1, 4)))
    out_weight = noise(streams_of[3], (QH * HD, D), (QH * HD) ** -0.5, 0.125, ((0, 4),))
    block_docs = jnp.searchsorted(jnp.cumsum(ragged_sizes(streams_of[4], DOCS, NBLK, MOST, 2)), jnp.arange(NBLK), side="right").astype(jnp.int32)
    return {"query_states": query_states, "key_states": key_states, "value_states": value_states, "out_weight": out_weight, "block_docs": block_docs}


def reference(query_states, key_states, value_states, out_weight, block_docs):
    group_size = QH // KH
    window = MOST * BLK
    score_scale = 1.0 / (HD ** 0.5)
    token_docs = jnp.repeat(block_docs, BLK, total_repeat_length=TOKENS)
    front = window - BLK
    key_padded = jnp.concatenate([jnp.zeros((front, KH * HD), key_states.dtype), key_states], axis=0)
    value_padded = jnp.concatenate([jnp.zeros((front, KH * HD), value_states.dtype), value_states], axis=0)
    docs_padded = jnp.concatenate([jnp.full((front,), -1, jnp.int32), token_docs.astype(jnp.int32)], axis=0)

    def one_block(block_index):
        start = (block_index * BLK).astype(jnp.int32)
        queries = lax.dynamic_slice_in_dim(query_states, start, BLK, 0).astype(jnp.float32).reshape(BLK, KH, group_size, HD)
        keys_here = lax.dynamic_slice_in_dim(key_padded, start, window, 0).astype(jnp.float32).reshape(window, KH, HD)
        values_here = lax.dynamic_slice_in_dim(value_padded, start, window, 0).astype(jnp.float32).reshape(window, KH, HD)
        query_docs = lax.dynamic_slice_in_dim(token_docs, start, BLK, 0)
        key_docs = lax.dynamic_slice_in_dim(docs_padded, start, window, 0)
        query_pos = start + jnp.arange(BLK, dtype=jnp.int32)
        key_pos = start - front + jnp.arange(window, dtype=jnp.int32)
        allowed = (query_docs[:, None] == key_docs[None, :]) & (key_pos[None, :] <= query_pos[:, None])
        scores = jnp.einsum("qgrd,kgd->grqk", queries, keys_here) * score_scale
        scores = jnp.where(allowed, scores, jnp.float32(-1e30))
        top = jnp.max(scores, axis=-1)
        weights = jnp.where(allowed, jnp.exp(scores - top[..., None]), jnp.float32(0.0))
        denominator = jnp.sum(weights, axis=-1)
        rounded = weights.astype(jnp.bfloat16).astype(jnp.float32)
        numerator = jnp.einsum("grqk,kgd->grqd", rounded, values_here)
        normalized = (numerator / denominator[..., None]).astype(jnp.bfloat16)
        return normalized.transpose(2, 0, 1, 3).reshape(BLK, QH * HD)

    attended = lax.map(one_block, jnp.arange(NBLK, dtype=jnp.int32)).reshape(TOKENS, QH * HD)
    group_width = QH * HD // N_HEAD

    def project(row_index):
        row_block = lax.dynamic_slice_in_dim(attended, (row_index * TOK_DEV).astype(jnp.int32), TOK_DEV, 0)
        summed = jnp.zeros((TOK_DEV, D), jnp.float32)
        for group in range(N_HEAD):
            partial_value = jnp.dot(row_block[:, group * group_width:(group + 1) * group_width], out_weight[group * group_width:(group + 1) * group_width], preferred_element_type=jnp.float32).astype(jnp.bfloat16)
            partial_value = lax.optimization_barrier(partial_value)
            summed = summed + partial_value.astype(jnp.float32)
        return summed.astype(jnp.bfloat16)

    return lax.map(project, jnp.arange(N_SEQ, dtype=jnp.int32)).reshape(TOKENS, D)
```

```python
import functools

import jax
import jax.numpy as jnp
from jax import lax
from jax.experimental import pallas as pl
from jax.experimental.pallas import tpu as pltpu
from jax.sharding import PartitionSpec as P

HD = 128
BLK = 128
GROUP = 4
HOPS = 8
JUMP = 4 * HOPS
COEF = 1.4426950408889634 / HD**0.5
FAR = 1e30
MESH = pl.DeviceIdType.MESH


def kernel(
    docs, q_hbm, k_hbm, v_hbm, w_hbm, out,
    q_in, qs, kb, vb, wv, acc, row_max, row_sum, att,
    p_out, p_in,
    loc_sem, send_sem, recv_sem, rs_send, rs_recv,
):
    s = lax.axis_index("seq")
    y = lax.axis_index("head")
    n = lax.axis_size("seq")
    heads = lax.axis_size("head")
    rows = BLK * GROUP
    width = wv.shape[2]
    half = width // 2
    fwd = lax.rem(s + 2, n)
    bwd = lax.rem(s + n - 2, n)
    far = lax.rem(s + JUMP, n)
    near = lax.rem(s + n - JUMP, n)
    mate = s + 1 - 2 * lax.rem(s, 2)
    up = lax.rem(y + 1, heads)
    down = lax.rem(y + heads - 1, heads)
    across = lax.rem(y + 2, heads)

    k_load = pltpu.make_async_copy(k_hbm, kb.at[0], loc_sem.at[0])
    v_load = pltpu.make_async_copy(v_hbm, vb.at[0], loc_sem.at[1])
    q_load = pltpu.make_async_copy(q_hbm, q_in, loc_sem.at[2])
    k_load.start()
    v_load.start()
    q_load.start()

    barrier = pltpu.get_barrier_semaphore()
    for peer in (fwd, bwd, far, near, mate):
        pl.semaphore_signal(barrier, inc=1, device_id={"seq": peer}, device_id_type=MESH)
    for peer in (up, down):
        pl.semaphore_signal(barrier, inc=1, device_id={"head": peer}, device_id_type=MESH)

    w_loads = []
    for i, dest in enumerate((across, up, down, y)):
        columns = pl.ds(pl.multiple_of(dest * width, width), width)
        load = pltpu.make_async_copy(w_hbm.at[:, columns], wv.at[i], loc_sem.at[3 + i])
        load.start()
        w_loads.append(load)
    pl.semaphore_wait(barrier, 7)

    def hop(t, kind, part):
        buf = (kb, vb)[part]
        if kind in (0, 2) or (isinstance(t, int) and t == 0):
            src = 4 * t
        else:
            src = 4 * t + 1
        if kind == 0:
            peer = fwd
        elif kind == 1:
            peer = far if (isinstance(t, int) and t == 0) else bwd
        else:
            peer = mate
        return pltpu.make_async_remote_copy(
            src_ref=buf.at[src],
            dst_ref=buf.at[4 * (t + 1) + kind],
            send_sem=send_sem.at[t, kind, part],
            recv_sem=recv_sem.at[t + 1, kind, part],
            device_id={"seq": peer},
            device_id_type=MESH,
        )

    def penalty(distance):
        other = s - distance
        same = docs[jnp.maximum(other, 0)] == docs[s]
        return jnp.where(same & (other >= 0) & (distance > 0), 0.0, FAR).astype(jnp.float32)

    def absorb(first, count, penalties):
        keys = kb[pl.ds(first, count)].reshape(count * BLK, HD)
        values = vb[pl.ds(first, count)].reshape(count * BLK, HD)
        scores = lax.dot_general(
            keys, qs[...], (((1,), (1,)), ((), ())), preferred_element_type=jnp.float32
        )
        parts = [scores[i * BLK:(i + 1) * BLK] for i in range(count)]
        old = row_max[...]
        new = old
        for part, pen in zip(parts, penalties):
            new = jnp.maximum(new, jnp.max(part, axis=0, keepdims=True) - pen)
        factor = jnp.exp2((old - new) * COEF)
        total = row_sum[...] * factor
        weights = []
        for part, pen in zip(parts, penalties):
            weight = jnp.exp2((part - (new + pen)) * COEF)
            total = total + jnp.sum(weight, axis=0, keepdims=True)
            weights.append(weight.astype(jnp.bfloat16))
        product = lax.dot_general(
            values, jnp.concatenate(weights, axis=0), (((0,), (0,)), ((), ())),
            preferred_element_type=jnp.float32,
        )
        acc[...] = acc[...] * factor + product
        row_max[...] = new
        row_sum[...] = total

    k_load.wait()
    for kind in (0, 1, 2):
        hop(0, kind, 0).start()
    v_load.wait()
    for kind in (0, 1, 2):
        hop(0, kind, 1).start()

    q_load.wait()
    for g in range(GROUP):
        qs[g * BLK:(g + 1) * BLK, :] = q_in[:, g * HD:(g + 1) * HD]

    scores = lax.dot_general(
        kb[0], qs[...], (((1,), (1,)), ((), ())), preferred_element_type=jnp.float32
    )
    key_at = lax.broadcasted_iota(jnp.int32, (BLK, rows), 0)
    query_at = lax.rem(lax.broadcasted_iota(jnp.int32, (BLK, rows), 1), BLK)
    scores = jnp.where(key_at <= query_at, scores, -FAR)
    top = jnp.max(scores, axis=0, keepdims=True)
    weight = jnp.exp2((scores - top) * COEF)
    row_max[...] = top
    row_sum[...] = jnp.sum(weight, axis=0, keepdims=True)
    acc[...] = lax.dot_general(
        vb[0], weight.astype(jnp.bfloat16), (((0,), (0,)), ((), ())),
        preferred_element_type=jnp.float32,
    )

    skew = 2 * lax.rem(s, 2) - 1

    def arrive(t, kinds, onward):
        for part in (0, 1):
            for kind in kinds:
                hop(t - 1, kind, part).wait_recv()
                if onward:
                    hop(t, kind, part).start()
                hop(t, kind + 2, part).start()

    arrive(1, (0, 1), True)
    for part in (0, 1):
        hop(0, 2, part).wait_recv()
    absorb(4, 3, [penalty(2), penalty(4 * HOPS), penalty(skew)])

    def middle(t, onward):
        arrive(t, (0, 1), onward)
        for part in (0, 1):
            for kind in (2, 3):
                hop(t - 1, kind, part).wait_recv()
        absorb(
            4 * t, 4,
            [
                penalty(2 * t),
                penalty(4 * HOPS + 2 - 2 * t),
                penalty(2 * (t - 1) + skew),
                penalty(4 * HOPS + 4 - 2 * t + skew),
            ],
        )

    @pl.loop(2, HOPS)
    def _(t):
        middle(t, True)

    middle(HOPS, False)
    for part in (0, 1):
        for kind in (2, 3):
            hop(HOPS, kind, part).wait_recv()
    absorb(
        4 * (HOPS + 1) + 2, 2,
        [penalty(2 * HOPS + skew), penalty(2 * HOPS + 2 + skew)],
    )

    scaled = acc[...] / row_sum[...]
    for g in range(GROUP):
        att[:, g * HD:(g + 1) * HD] = scaled[:, g * BLK:(g + 1) * BLK].T.astype(jnp.bfloat16)

    def project(i, side):
        return jnp.dot(
            att[...], wv[i, :, side * half:(side + 1) * half],
            preferred_element_type=jnp.float32,
        )

    def give(stage, side):
        return pltpu.make_async_remote_copy(
            src_ref=p_out.at[stage, side],
            dst_ref=p_in.at[stage, side],
            send_sem=rs_send.at[stage, side],
            recv_sem=rs_recv.at[stage, side],
            device_id={"head": up if side == 0 else down},
            device_id_type=MESH,
        )

    w_loads[0].wait()
    for side in (0, 1):
        p_out[0, side] = project(0, side).astype(jnp.bfloat16)
        give(0, side).start()
    w_loads[1].wait()
    w_loads[2].wait()
    for side in (0, 1):
        p_out[1, side] = project(1 + side, 1 - side).astype(jnp.bfloat16)
        give(1, side).start()
    held = [project(1 + side, side) for side in (0, 1)]
    for side in (0, 1):
        give(0, side).wait_recv()
        p_out[2, side] = (held[side] + p_in[0, side].astype(jnp.float32)).astype(jnp.bfloat16)
        give(2, side).start()
    w_loads[3].wait()
    own = [project(3, side) for side in (0, 1)]
    for side in (0, 1):
        give(1, 1 - side).wait_recv()
        own[side] = own[side] + p_in[1, 1 - side].astype(jnp.float32)
    for side in (0, 1):
        give(2, side).wait_recv()
        out[:, side * half:(side + 1) * half] = (
            own[side] + p_in[2, side].astype(jnp.float32)
        ).astype(jnp.bfloat16)

    for part in (0, 1):
        for kind in (0, 1, 2):
            hop(0, kind, part).wait_send()

    @pl.loop(1, HOPS)
    def _(t):
        for part in (0, 1):
            for kind in (0, 1, 2, 3):
                hop(t, kind, part).wait_send()

    for part in (0, 1):
        for kind in (2, 3):
            hop(HOPS, kind, part).wait_send()
    for stage in (0, 1, 2):
        for side in (0, 1):
            give(stage, side).wait_send()


def local(query_states, key_states, value_states, out_weight, block_docs):
    tokens = query_states.shape[0]
    model = out_weight.shape[1]
    width = model // lax.axis_size("head")
    rows = GROUP * BLK
    any_space = pl.BlockSpec(memory_space=pl.ANY)
    return pl.pallas_call(
        kernel,
        out_shape=jax.ShapeDtypeStruct((tokens, width), jnp.bfloat16),
        in_specs=[pl.BlockSpec(memory_space=pltpu.SMEM)] + [any_space] * 4,
        out_specs=pl.BlockSpec(memory_space=pltpu.VMEM),
        scratch_shapes=[
            pltpu.VMEM((tokens, rows), jnp.bfloat16),
            pltpu.VMEM((rows, HD), jnp.bfloat16),
            pltpu.VMEM((4 * (HOPS + 2), BLK, HD), jnp.bfloat16),
            pltpu.VMEM((4 * (HOPS + 2), BLK, HD), jnp.bfloat16),
            pltpu.VMEM((4, rows, width), jnp.bfloat16),
            pltpu.VMEM((HD, rows), jnp.float32),
            pltpu.VMEM((1, rows), jnp.float32),
            pltpu.VMEM((1, rows), jnp.float32),
            pltpu.VMEM((tokens, rows), jnp.bfloat16),
            pltpu.VMEM((3, 2, tokens, width // 2), jnp.bfloat16),
            pltpu.VMEM((3, 2, tokens, width // 2), jnp.bfloat16),
            pltpu.SemaphoreType.DMA((7,)),
            pltpu.SemaphoreType.DMA((HOPS + 1, 4, 2)),
            pltpu.SemaphoreType.DMA((HOPS + 2, 4, 2)),
            pltpu.SemaphoreType.DMA((3, 2)),
            pltpu.SemaphoreType.DMA((3, 2)),
        ],
        compiler_params=pltpu.CompilerParams(
            collective_id=0, has_side_effects=True, vmem_limit_bytes=60 << 20
        ),
    )(block_docs, query_states, key_states, value_states, out_weight)


def solution(mesh):
    return jax.shard_map(
        local,
        mesh=mesh,
        in_specs=(P("seq", "head"), P("seq", "head"), P("seq", "head"), P("head", None), P()),
        out_specs=P("seq", "head"),
        check_vma=False,
    )
```

```python
import functools

import jax
import jax.numpy as jnp
from jax import lax
from jax.experimental import pallas as pl
from jax.experimental.pallas import tpu as pltpu
from jax.sharding import PartitionSpec as P

HD = 128
BLK = 128
GROUP = 4
EDGES = ((0, 2), (0, 14), (0, 1), (0, 15), (0, 16), (2, 4), (14, 12), (4, 6), (12, 10), (2, 3), (14, 13), (4, 5), (12, 11), (6, 7), (10, 9))
HALVES = ((6, 8, 0),)
SLOTS = (0, 16, 2, 14, 1, 15, 4, 12, 3, 13, 6, 10, 5, 11, 7, 9, 8)
CHUNKS = ((2, 14, 1, 15), (4, 12, 3, 13), (6, 10, 5, 11), (7, 9, 8))
PARTS = (0,)
COUNT = len(SLOTS)
SLOT = {chips: at for at, chips in enumerate(SLOTS)}
ROUTES = tuple((a, b, p) for a, b in EDGES for p in PARTS) + HALVES
STEPS = tuple(sorted({b - a for a, b, _ in ROUTES}))
COEF = 1.4426950408889634 / HD**0.5
FAR = 1e30
MESH = pl.DeviceIdType.MESH


def kernel(
    docs_hbm, q_hbm, k_hbm, v_hbm, w_hbm, out,
    q_in, qs, kv, wv, acc, row_max, row_sum, att,
    p_out, p_in,
    docs, loc_sem, send_sem, share_send, recv_sem, rs_send, rs_recv,
):
    s = lax.axis_index("seq")
    y = lax.axis_index("head")
    n = lax.axis_size("seq")
    heads = lax.axis_size("head")
    rows = BLK * GROUP
    width = wv.shape[2]
    half = width // 2
    reach = {step: lax.rem(s + n + 2 * step, n) for step in STEPS}
    back = {step: lax.rem(s + n - 2 * step, n) for step in STEPS if -step not in STEPS}
    mate = s + 1 - 2 * lax.rem(s, 2)
    up = lax.rem(y + 1, heads)
    down = lax.rem(y + heads - 1, heads)
    across = lax.rem(y + 2, heads)

    k_load = pltpu.make_async_copy(k_hbm, kv.at[0, 0], loc_sem.at[0])
    v_load = pltpu.make_async_copy(v_hbm, kv.at[0, 1], loc_sem.at[1])
    q_load = pltpu.make_async_copy(q_hbm, q_in, loc_sem.at[2])
    docs_load = pltpu.make_async_copy(docs_hbm, docs, loc_sem.at[7])
    docs_load.start()
    k_load.start()
    v_load.start()
    q_load.start()

    barrier = pltpu.get_barrier_semaphore()
    for peer in (*reach.values(), *back.values(), mate):
        pl.semaphore_signal(barrier, inc=1, device_id={"seq": peer}, device_id_type=MESH)
    for peer in (up, down):
        pl.semaphore_signal(barrier, inc=1, device_id={"head": peer}, device_id_type=MESH)

    w_loads = []
    for i, dest in enumerate((across, up, down, y)):
        columns = pl.ds(pl.multiple_of(dest * width, width), width)
        load = pltpu.make_async_copy(w_hbm.at[:, columns], wv.at[i], loc_sem.at[3 + i])
        load.start()
        w_loads.append(load)
    pl.semaphore_wait(barrier, len(reach) + len(back) + 3)

    def send(frm, to, part):
        buf = kv
        route = ROUTES.index((frm, to, part))
        return pltpu.make_async_remote_copy(
            src_ref=buf.at[SLOT[frm]],
            dst_ref=buf.at[SLOT[to]],
            send_sem=send_sem.at[route],
            recv_sem=recv_sem.at[SLOT[to], part],
            device_id={"seq": reach[to - frm]},
            device_id_type=MESH,
        )

    def share(chips, part):
        buf = kv
        return pltpu.make_async_remote_copy(
            src_ref=buf.at[SLOT[chips]],
            dst_ref=buf.at[COUNT + SLOT[chips]],
            send_sem=share_send.at[SLOT[chips], part],
            recv_sem=recv_sem.at[COUNT + SLOT[chips], part],
            device_id={"seq": mate},
            device_id_type=MESH,
        )

    def spread(chips, part):
        for a, b, p in ROUTES:
            if (a, p) == (chips, part):
                send(a, b, p).start()

    parent = {(b, p): a for a, b, p in ROUTES}

    def arrive(*chips):
        for c in chips:
            for part in PARTS:
                send(parent[c, part], c, part).wait_recv()
                spread(c, part)
            for part in PARTS:
                share(c, part).start()

    def shared(*chips):
        for c in chips:
            for part in PARTS:
                share(c, part).wait_recv()

    def penalty(distance):
        other = s - distance
        same = docs[jnp.maximum(other, 0)] == docs[s]
        return jnp.where(same & (other >= 0) & (distance > 0), 0.0, FAR).astype(jnp.float32)

    def absorb(first, count, penalties):
        keys = kv[first:first + count, 0].reshape(count * BLK, HD)
        values = kv[first:first + count, 1].reshape(count * BLK, HD)
        scores = lax.dot_general(
            keys, qs[...], (((1,), (1,)), ((), ())), preferred_element_type=jnp.float32
        )
        parts = [scores[i * BLK:(i + 1) * BLK] for i in range(count)]
        old = row_max[...]
        new = old
        for part, pen in zip(parts, penalties):
            new = jnp.maximum(new, jnp.max(part, axis=0, keepdims=True) - pen)
        factor = jnp.exp2((old - new) * COEF)
        total = row_sum[...] * factor
        weights = []
        for part, pen in zip(parts, penalties):
            weight = jnp.exp2((part - (new + pen)) * COEF)
            total = total + jnp.sum(weight, axis=0, keepdims=True)
            weights.append(weight.astype(jnp.bfloat16))
        product = lax.dot_general(
            values, jnp.concatenate(weights, axis=0), (((0,), (0,)), ((), ())),
            preferred_element_type=jnp.float32,
        )
        acc[...] = acc[...] * factor + product
        row_max[...] = new
        row_sum[...] = total

    k_load.wait()
    v_load.wait()
    spread(0, 0)
    for part in PARTS:
        share(0, part).start()

    docs_load.wait()
    q_load.wait()
    for g in range(GROUP):
        qs[g * BLK:(g + 1) * BLK, :] = q_in[:, g * HD:(g + 1) * HD]

    scores = lax.dot_general(
        kv[0, 0], qs[...], (((1,), (1,)), ((), ())), preferred_element_type=jnp.float32
    )
    key_at = lax.broadcasted_iota(jnp.int32, (BLK, rows), 0)
    query_at = lax.rem(lax.broadcasted_iota(jnp.int32, (BLK, rows), 1), BLK)
    scores = jnp.where(key_at <= query_at, scores, -FAR)
    top = jnp.max(scores, axis=0, keepdims=True)
    weight = jnp.exp2((scores - top) * COEF)
    row_max[...] = top
    row_sum[...] = jnp.sum(weight, axis=0, keepdims=True)
    acc[...] = lax.dot_general(
        kv[0, 1], weight.astype(jnp.bfloat16), (((0,), (0,)), ((), ())),
        preferred_element_type=jnp.float32,
    )

    skew = 2 * lax.rem(s, 2) - 1

    def mine(chips):
        absorb(SLOT[chips[0]], len(chips), [penalty(2 * c) for c in chips])

    def other(chips):
        shared(*chips)
        absorb(COUNT + SLOT[chips[0]], len(chips), [penalty(2 * c + skew) for c in chips])

    arrive(*CHUNKS[0], 16)
    mine(CHUNKS[0])
    arrive(*CHUNKS[1])
    other((0, 16))
    other(CHUNKS[0])
    mine(CHUNKS[1])
    arrive(*CHUNKS[2])
    other(CHUNKS[1])
    mine(CHUNKS[2])
    arrive(*CHUNKS[3])
    mine(CHUNKS[3])
    other(CHUNKS[2])
    other(CHUNKS[3])

    scaled = acc[...] / row_sum[...]
    for g in range(GROUP):
        att[:, g * HD:(g + 1) * HD] = scaled[:, g * BLK:(g + 1) * BLK].T.astype(jnp.bfloat16)

    def project(i, side):
        return jnp.dot(
            att[...], wv[i, :, side * half:(side + 1) * half],
            preferred_element_type=jnp.float32,
        )

    def give(stage, side):
        return pltpu.make_async_remote_copy(
            src_ref=p_out.at[stage, side],
            dst_ref=p_in.at[stage, side],
            send_sem=rs_send.at[stage, side],
            recv_sem=rs_recv.at[stage, side],
            device_id={"head": up if side == 0 else down},
            device_id_type=MESH,
        )

    w_loads[0].wait()
    for side in (0, 1):
        p_out[0, side] = project(0, side).astype(jnp.bfloat16)
        give(0, side).start()
    w_loads[1].wait()
    w_loads[2].wait()
    for side in (0, 1):
        p_out[1, side] = project(1 + side, 1 - side).astype(jnp.bfloat16)
        give(1, side).start()
    held = [project(1 + side, side) for side in (0, 1)]
    for side in (0, 1):
        give(0, side).wait_recv()
        p_out[2, side] = (held[side] + p_in[0, side].astype(jnp.float32)).astype(jnp.bfloat16)
        give(2, side).start()
    w_loads[3].wait()
    own = [project(3, side) for side in (0, 1)]
    for side in (0, 1):
        give(1, 1 - side).wait_recv()
        own[side] = own[side] + p_in[1, 1 - side].astype(jnp.float32)
    for side in (0, 1):
        give(2, side).wait_recv()
        out[:, side * half:(side + 1) * half] = (
            own[side] + p_in[2, side].astype(jnp.float32)
        ).astype(jnp.bfloat16)

    for route in ROUTES:
        send(*route).wait_send()
    for chips in SLOTS:
        for part in PARTS:
            share(chips, part).wait_send()
    for stage in (0, 1, 2):
        for side in (0, 1):
            give(stage, side).wait_send()


def local(query_states, key_states, value_states, out_weight, block_docs):
    query_states, key_states, value_states, out_weight, block_docs = [pltpu.with_memory_space_constraint(a, pltpu.HBM) for a in (query_states, key_states, value_states, out_weight, block_docs)]
    tokens = query_states.shape[0]
    model = out_weight.shape[1]
    width = model // lax.axis_size("head")
    rows = GROUP * BLK
    any_space = pl.BlockSpec(memory_space=pltpu.HBM)
    return pl.pallas_call(
        kernel,
        out_shape=jax.ShapeDtypeStruct((tokens, width), jnp.bfloat16),
        in_specs=[any_space] * 5,
        out_specs=pl.BlockSpec(memory_space=pltpu.VMEM),
        scratch_shapes=[
            pltpu.VMEM((tokens, rows), jnp.bfloat16),
            pltpu.VMEM((rows, HD), jnp.bfloat16),
            pltpu.VMEM((2 * COUNT, 2, BLK, HD), jnp.bfloat16),
            pltpu.VMEM((4, rows, width), jnp.bfloat16),
            pltpu.VMEM((HD, rows), jnp.float32),
            pltpu.VMEM((1, rows), jnp.float32),
            pltpu.VMEM((1, rows), jnp.float32),
            pltpu.VMEM((tokens, rows), jnp.bfloat16),
            pltpu.VMEM((3, 2, tokens, width // 2), jnp.bfloat16),
            pltpu.VMEM((3, 2, tokens, width // 2), jnp.bfloat16),
            pltpu.SMEM((128,), jnp.int32),
            pltpu.SemaphoreType.DMA((8,)),
            pltpu.SemaphoreType.DMA((len(ROUTES),)),
            pltpu.SemaphoreType.DMA((COUNT, 2)),
            pltpu.SemaphoreType.DMA((2 * COUNT, 2)),
            pltpu.SemaphoreType.DMA((3, 2)),
            pltpu.SemaphoreType.DMA((3, 2)),
        ],
        compiler_params=pltpu.CompilerParams(
            collective_id=0, has_side_effects=True, vmem_limit_bytes=20 << 20
        ),
    )(block_docs, query_states, key_states, value_states, out_weight)


def solution(mesh):
    return jax.shard_map(
        local,
        mesh=mesh,
        in_specs=(P("seq", "head"), P("seq", "head"), P("seq", "head"), P("head", None), P()),
        out_specs=P("seq", "head"),
        check_vma=False,
    )
```

```python
import functools

import jax
import jax.numpy as jnp
from jax import lax
from jax.experimental import pallas as pl
from jax.experimental.pallas import tpu as pltpu
from jax.sharding import PartitionSpec as P

HD = 128
BLK = 128
GROUP = 4
CHAIN = ((0, 2), (0, 14), (2, 4), (14, 12), (4, 6), (12, 10))
LEAVES = (
    (0, 1), (0, 15), (0, 16),
    (2, 3), (14, 13), (4, 5), (12, 11), (6, 7), (10, 9),
)
LAST = ((6, 8, 0), (10, 8, 1))
SLOTS = (0, 16, 2, 14, 1, 15, 4, 12, 3, 13, 6, 10, 5, 11, 7, 9, 8)
OWN, UP, DOWN, ACROSS = range(4)
CHUNKS = ((2, 14, 1, 15), (4, 12, 3, 13), (6, 10, 5, 11), (7, 9, 8))
COUNT = len(SLOTS)
SLOT = {chips: at for at, chips in enumerate(SLOTS)}
ROUTES = tuple((a, b, p) for a, b in CHAIN for p in (0, 1)) + LAST + tuple((a, b, 2) for a, b in LEAVES)
PARENT = {(b, p): a for a, b, p in ROUTES}
STEPS = tuple(sorted({b - a for a, b, _ in ROUTES}))
COEF = 1.4426950408889634 / HD**0.5
FAR = 1e30
MESH = pl.DeviceIdType.MESH


def kernel(
    docs_hbm, q_hbm, k_hbm, v_hbm, w_hbm, out,
    q_in, qs, kv, wx, transit, acc, row_max, row_sum, att, ax, mixed,
    docs, loc_sem, send_sem, share_send, recv_sem, share_recv, w_send, w_recv, a_send, a_recv,
):
    s = lax.axis_index("seq")
    y = lax.axis_index("head")
    n = lax.axis_size("seq")
    heads = lax.axis_size("head")
    rows = BLK * GROUP
    width = wx.shape[2]
    side_rows = rows // 2
    quarter = rows // 4
    token_half = BLK // 2
    reach = {step: lax.rem(s + n + 2 * step, n) for step in STEPS}
    back = {step: lax.rem(s + n - 2 * step, n) for step in STEPS if -step not in STEPS}
    mate = s + 1 - 2 * lax.rem(s, 2)
    up = lax.rem(y + 1, heads)
    down = lax.rem(y + heads - 1, heads)
    across = lax.rem(y + 2, heads)

    k_load = pltpu.make_async_copy(k_hbm, kv.at[0, 0], loc_sem.at[0])
    v_load = pltpu.make_async_copy(v_hbm, kv.at[0, 1], loc_sem.at[1])
    q_load = pltpu.make_async_copy(q_hbm, q_in, loc_sem.at[2])
    docs_load = pltpu.make_async_copy(docs_hbm, docs, loc_sem.at[4])
    docs_load.start()
    k_load.start()
    v_load.start()
    q_load.start()

    barrier = pltpu.get_barrier_semaphore()
    for peer in (*reach.values(), *back.values(), mate):
        pl.semaphore_signal(barrier, inc=1, device_id={"seq": peer}, device_id_type=MESH)
    for peer in (up, down):
        pl.semaphore_signal(barrier, inc=1, device_id={"head": peer}, device_id_type=MESH)

    def columns(dest):
        return pl.ds(pl.multiple_of(dest * width, width), width)

    w_own = pltpu.make_async_copy(w_hbm.at[:, columns(y)], wx.at[OWN], loc_sem.at[3])
    w_own.start()
    pl.semaphore_wait(barrier, len(reach) + len(back) + 3)

    def view(slot, part):
        return kv.at[slot] if part == 2 else kv.at[slot, part]

    def send(frm, to, part):
        route = ROUTES.index((frm, to, part))
        return pltpu.make_async_remote_copy(
            src_ref=view(SLOT[frm], part),
            dst_ref=view(SLOT[to], part),
            send_sem=send_sem.at[route],
            recv_sem=recv_sem.at[SLOT[to], part],
            device_id={"seq": reach[to - frm]},
            device_id_type=MESH,
        )

    def share(chips):
        return pltpu.make_async_remote_copy(
            src_ref=kv.at[SLOT[chips]],
            dst_ref=kv.at[COUNT + SLOT[chips]],
            send_sem=share_send.at[SLOT[chips]],
            recv_sem=share_recv.at[SLOT[chips]],
            device_id={"seq": mate},
            device_id_type=MESH,
        )

    def spread(chips, part):
        for a, b, p in ROUTES:
            if (a, p) == (chips, part):
                send(a, b, p).start()

    def arrive(*chips):
        for c in chips:
            for part in (0, 1, 2):
                if (c, part) in PARENT:
                    send(PARENT[c, part], c, part).wait_recv()
                    if part < 2:
                        spread(c, part)
            spread(c, 2)
            share(c).start()

    def shared(*chips):
        for c in chips:
            share(c).wait_recv()

    first_row = pl.multiple_of(lax.rem(s, 2) * side_rows, side_rows)

    def over(side, src, dst, at):
        return pltpu.make_async_remote_copy(
            src_ref=src, dst_ref=dst, send_sem=w_send.at[at], recv_sem=w_recv.at[at],
            device_id={"head": up if side == 0 else down}, device_id_type=MESH,
        )

    def w_first(side):
        span = pl.ds(first_row + side * quarter, quarter)
        return over(side, w_hbm.at[span, columns(across)], transit.at[side], side)

    def w_direct(side):
        span = pl.ds(first_row, side_rows)
        dest = up if side == 0 else down
        return over(side, w_hbm.at[span, columns(dest)], wx.at[DOWN - side, span], 2 + side)

    def w_onward(side):
        span = pl.ds(first_row + side * quarter, quarter)
        return over(side, transit.at[side], wx.at[ACROSS, span], 4 + side)

    def w_share(group):
        span = pl.ds(first_row, side_rows)
        return pltpu.make_async_remote_copy(
            src_ref=wx.at[group, span], dst_ref=wx.at[group, span],
            send_sem=w_send.at[5 + group], recv_sem=w_recv.at[5 + group],
            device_id={"seq": mate}, device_id_type=MESH,
        )

    def penalty(distance):
        other = s - distance
        same = docs[jnp.maximum(other, 0)] == docs[s]
        return jnp.where(same & (other >= 0) & (distance > 0), 0.0, FAR).astype(jnp.float32)

    def absorb(first, count, penalties):
        keys = kv[first:first + count, 0].reshape(count * BLK, HD)
        values = kv[first:first + count, 1].reshape(count * BLK, HD)
        scores = lax.dot_general(
            keys, qs[...], (((1,), (1,)), ((), ())), preferred_element_type=jnp.float32
        )
        parts = [scores[i * BLK:(i + 1) * BLK] for i in range(count)]
        old = row_max[...]
        new = old
        for part, pen in zip(parts, penalties):
            new = jnp.maximum(new, jnp.max(part, axis=0, keepdims=True) - pen)
        factor = jnp.exp2((old - new) * COEF)
        total = row_sum[...] * factor
        weights = []
        for part, pen in zip(parts, penalties):
            weight = jnp.exp2((part - (new + pen)) * COEF)
            total = total + jnp.sum(weight, axis=0, keepdims=True)
            weights.append(weight.astype(jnp.bfloat16))
        product = lax.dot_general(
            values, jnp.concatenate(weights, axis=0), (((0,), (0,)), ((), ())),
            preferred_element_type=jnp.float32,
        )
        acc[...] = acc[...] * factor + product
        row_max[...] = new
        row_sum[...] = total

    k_load.wait()
    spread(0, 0)
    v_load.wait()
    spread(0, 1)
    spread(0, 2)
    share(0).start()
    for side in (0, 1):
        w_first(side).start()
    for side in (0, 1):
        w_direct(side).start()

    docs_load.wait()
    q_load.wait()
    for g in range(GROUP):
        qs[g * BLK:(g + 1) * BLK, :] = q_in[:, g * HD:(g + 1) * HD]

    scores = lax.dot_general(
        kv[0, 0], qs[...], (((1,), (1,)), ((), ())), preferred_element_type=jnp.float32
    )
    key_at = lax.broadcasted_iota(jnp.int32, (BLK, rows), 0)
    query_at = lax.rem(lax.broadcasted_iota(jnp.int32, (BLK, rows), 1), BLK)
    scores = jnp.where(key_at <= query_at, scores, -FAR)
    top = jnp.max(scores, axis=0, keepdims=True)
    weight = jnp.exp2((scores - top) * COEF)
    row_max[...] = top
    row_sum[...] = jnp.sum(weight, axis=0, keepdims=True)
    acc[...] = lax.dot_general(
        kv[0, 1], weight.astype(jnp.bfloat16), (((0,), (0,)), ((), ())),
        preferred_element_type=jnp.float32,
    )

    skew = 2 * lax.rem(s, 2) - 1

    def mine(chips):
        absorb(SLOT[chips[0]], len(chips), [penalty(2 * c) for c in chips])

    def other(chips):
        shared(*chips)
        absorb(COUNT + SLOT[chips[0]], len(chips), [penalty(2 * c + skew) for c in chips])

    arrive(*CHUNKS[0], 16)
    mine(CHUNKS[0])
    arrive(*CHUNKS[1])
    for side in (0, 1):
        w_first(side).wait_recv()
        w_onward(side).start()
    other((0, 16))
    other(CHUNKS[0])
    mine(CHUNKS[1])
    arrive(*CHUNKS[2])
    other(CHUNKS[1])
    mine(CHUNKS[2])
    arrive(*CHUNKS[3])
    mine(CHUNKS[3])
    other(CHUNKS[2])
    for side in (0, 1):
        w_direct(side).wait_recv()
        w_share(DOWN - side).start()
    other(CHUNKS[3])

    scaled = acc[...] / row_sum[...]
    for g in range(GROUP):
        att[:, g * HD:(g + 1) * HD] = scaled[:, g * BLK:(g + 1) * BLK].T.astype(jnp.bfloat16)

    def a_give(side, piece):
        span = pl.ds(piece * token_half, token_half)
        return pltpu.make_async_remote_copy(
            src_ref=att.at[span], dst_ref=ax.at[1 - side, span],
            send_sem=a_send.at[side, piece], recv_sem=a_recv.at[side, piece],
            device_id={"head": up if side == 0 else down}, device_id_type=MESH,
        )

    def a_onward(side):
        span = pl.ds(side * token_half, token_half)
        return pltpu.make_async_remote_copy(
            src_ref=ax.at[1 - side, span], dst_ref=ax.at[2, span],
            send_sem=a_send.at[side, 2], recv_sem=a_recv.at[side, 2],
            device_id={"head": up if side == 0 else down}, device_id_type=MESH,
        )

    for side, piece in ((0, 0), (1, 1), (0, 1), (1, 0)):
        a_give(side, piece).start()
    w_own.wait()
    mixed[...] = jnp.dot(att[...], wx[OWN], preferred_element_type=jnp.float32)
    for side in (0, 1):
        a_give(side, side).wait_recv()
        a_onward(side).start()
    for side in (0, 1):
        w_onward(side).wait_recv()
    w_share(ACROSS).start()
    for side in (0, 1):
        a_give(side, 1 - side).wait_recv()
        w_share(DOWN - side).wait_recv()
        mixed[...] += jnp.dot(ax[1 - side], wx[DOWN - side], preferred_element_type=jnp.float32)
    w_share(ACROSS).wait_recv()
    for side in (0, 1):
        a_onward(side).wait_recv()
    out[...] = (
        mixed[...] + jnp.dot(ax[2], wx[ACROSS], preferred_element_type=jnp.float32)
    ).astype(jnp.bfloat16)

    for route in ROUTES:
        send(*route).wait_send()
    for chips in SLOTS:
        share(chips).wait_send()
    for side in (0, 1):
        w_first(side).wait_send()
        w_direct(side).wait_send()
        w_onward(side).wait_send()
        for piece in (0, 1):
            a_give(side, piece).wait_send()
        a_onward(side).wait_send()
    for group in (UP, DOWN, ACROSS):
        w_share(group).wait_send()


def local(query_states, key_states, value_states, out_weight, block_docs):
    query_states, key_states, value_states, out_weight, block_docs = [pltpu.with_memory_space_constraint(a, pltpu.HBM) for a in (query_states, key_states, value_states, out_weight, block_docs)]
    tokens = query_states.shape[0]
    model = out_weight.shape[1]
    width = model // lax.axis_size("head")
    rows = GROUP * BLK
    any_space = pl.BlockSpec(memory_space=pltpu.HBM)
    return pl.pallas_call(
        kernel,
        out_shape=jax.ShapeDtypeStruct((tokens, width), jnp.bfloat16),
        in_specs=[any_space] * 5,
        out_specs=pl.BlockSpec(memory_space=pltpu.VMEM),
        scratch_shapes=[
            pltpu.VMEM((tokens, rows), jnp.bfloat16),
            pltpu.VMEM((rows, HD), jnp.bfloat16),
            pltpu.VMEM((2 * COUNT, 2, BLK, HD), jnp.bfloat16),
            pltpu.VMEM((4, rows, width), jnp.bfloat16),
            pltpu.VMEM((2, rows // 4, width), jnp.bfloat16),
            pltpu.VMEM((HD, rows), jnp.float32),
            pltpu.VMEM((1, rows), jnp.float32),
            pltpu.VMEM((1, rows), jnp.float32),
            pltpu.VMEM((tokens, rows), jnp.bfloat16),
            pltpu.VMEM((3, tokens, rows), jnp.bfloat16),
            pltpu.VMEM((tokens, width), jnp.float32),
            pltpu.SMEM((128,), jnp.int32),
            pltpu.SemaphoreType.DMA((5,)),
            pltpu.SemaphoreType.DMA((len(ROUTES),)),
            pltpu.SemaphoreType.DMA((COUNT,)),
            pltpu.SemaphoreType.DMA((COUNT, 3)),
            pltpu.SemaphoreType.DMA((COUNT,)),
            pltpu.SemaphoreType.DMA((9,)),
            pltpu.SemaphoreType.DMA((9,)),
            pltpu.SemaphoreType.DMA((2, 3)),
            pltpu.SemaphoreType.DMA((2, 3)),
        ],
        compiler_params=pltpu.CompilerParams(
            collective_id=0, has_side_effects=True, vmem_limit_bytes=20 << 20
        ),
    )(block_docs, query_states, key_states, value_states, out_weight)


def solution(mesh):
    return jax.shard_map(
        local,
        mesh=mesh,
        in_specs=(P("seq", "head"), P("seq", "head"), P("seq", "head"), P("head", None), P()),
        out_specs=P("seq", "head"),
        check_vma=False,
    )
```

```python
import functools

import jax
import jax.numpy as jnp
from jax import lax
from jax.experimental import pallas as pl
from jax.experimental.pallas import tpu as pltpu
from jax.sharding import PartitionSpec as P

HD = 128
BLK = 128
GROUP = 4
CHAIN = ((0, 2), (0, 14), (2, 4), (14, 12), (4, 6), (12, 10))
LEAVES = (
    (0, 1), (0, 15), (0, 16),
    (2, 3), (14, 13), (4, 5), (12, 11), (6, 7), (10, 9),
)
LAST = ((6, 8, 0), (10, 8, 1))
SLOTS = (0, 16, 2, 14, 1, 15, 4, 12, 3, 13, 6, 10, 5, 11, 7, 9, 8)
OWN, UP, DOWN, ACROSS = range(4)
CHUNKS = ((2, 14, 1, 15), (4, 12, 3, 13), (6, 10, 5, 11), (7, 9, 8))
COUNT = len(SLOTS)
SLOT = {chips: at for at, chips in enumerate(SLOTS)}
PARTS = (0, 1)
WHOLE = 2
ROUTES = tuple((a, b, p) for a, b in CHAIN for p in PARTS) + LAST + tuple((a, b, WHOLE) for a, b in LEAVES)
PARENT = {(b, p): a for a, b, p in ROUTES}
STEPS = tuple(sorted({b - a for a, b, _ in ROUTES}))
COEF = 1.4426950408889634 / HD**0.5
FAR = 1e30
MESH = pl.DeviceIdType.MESH


def kernel(
    docs_hbm, q_hbm, k_hbm, v_hbm, w_hbm, out,
    q_in, qs, kv, wx, transit, acc, row_max, row_sum, att, ax, mixed,
    docs, loc_sem, send_sem, share_send, recv_sem, share_recv, w_send, w_recv, a_send, a_recv,
):
    s = lax.axis_index("seq")
    y = lax.axis_index("head")
    n = lax.axis_size("seq")
    heads = lax.axis_size("head")
    rows = BLK * GROUP
    width = wx.shape[2]
    side_rows = rows // 2
    quarter = rows // 4
    token_half = BLK // 2
    reach = {step: lax.rem(s + n + 2 * step, n) for step in STEPS}
    back = {step: lax.rem(s + n - 2 * step, n) for step in STEPS if -step not in STEPS}
    mate = s + 1 - 2 * lax.rem(s, 2)
    up = lax.rem(y + 1, heads)
    down = lax.rem(y + heads - 1, heads)
    across = lax.rem(y + 2, heads)

    k_load = pltpu.make_async_copy(k_hbm, kv.at[0, 0], loc_sem.at[0])
    v_load = pltpu.make_async_copy(v_hbm, kv.at[0, 1], loc_sem.at[1])
    q_load = pltpu.make_async_copy(q_hbm, q_in, loc_sem.at[2])
    docs_load = pltpu.make_async_copy(docs_hbm, docs, loc_sem.at[4])
    docs_load.start()
    k_load.start()
    v_load.start()
    q_load.start()

    barrier = pltpu.get_barrier_semaphore()
    for peer in (*reach.values(), *back.values(), mate):
        pl.semaphore_signal(barrier, inc=1, device_id={"seq": peer}, device_id_type=MESH)
    for peer in (up, down):
        pl.semaphore_signal(barrier, inc=1, device_id={"head": peer}, device_id_type=MESH)

    def columns(dest):
        return pl.ds(pl.multiple_of(dest * width, width), width)

    w_own = pltpu.make_async_copy(w_hbm.at[:, columns(y)], wx.at[OWN], loc_sem.at[3])
    w_own.start()
    pl.semaphore_wait(barrier, len(reach) + len(back) + 3)

    def view(slot, part):
        return kv.at[slot] if part == WHOLE else kv.at[slot, part]

    def send(frm, to, part):
        route = ROUTES.index((frm, to, part))
        return pltpu.make_async_remote_copy(
            src_ref=view(SLOT[frm], part),
            dst_ref=view(SLOT[to], part),
            send_sem=send_sem.at[route],
            recv_sem=recv_sem.at[SLOT[to], part],
            device_id={"seq": reach[to - frm]},
            device_id_type=MESH,
        )

    def share(chips):
        return pltpu.make_async_remote_copy(
            src_ref=kv.at[SLOT[chips]],
            dst_ref=kv.at[COUNT + SLOT[chips]],
            send_sem=share_send.at[SLOT[chips]],
            recv_sem=share_recv.at[SLOT[chips]],
            device_id={"seq": mate},
            device_id_type=MESH,
        )

    def spread(chips, part):
        for a, b, p in ROUTES:
            if (a, p) == (chips, part):
                send(a, b, p).start()

    def arrive(*chips):
        for part in PARTS:
            for c in chips:
                if (c, part) in PARENT:
                    send(PARENT[c, part], c, part).wait_recv()
                    spread(c, part)
        for c in chips:
            if (c, WHOLE) in PARENT:
                send(PARENT[c, WHOLE], c, WHOLE).wait_recv()
            spread(c, WHOLE)
            share(c).start()

    def shared(*chips):
        for c in chips:
            share(c).wait_recv()

    first_row = pl.multiple_of(lax.rem(s, 2) * side_rows, side_rows)

    def over(side, src, dst, at):
        return pltpu.make_async_remote_copy(
            src_ref=src, dst_ref=dst, send_sem=w_send.at[at], recv_sem=w_recv.at[at],
            device_id={"head": up if side == 0 else down}, device_id_type=MESH,
        )

    def w_first(side):
        span = pl.ds(first_row + side * quarter, quarter)
        return over(side, w_hbm.at[span, columns(across)], transit.at[side], side)

    def w_direct(side):
        span = pl.ds(first_row, side_rows)
        dest = up if side == 0 else down
        return over(side, w_hbm.at[span, columns(dest)], wx.at[DOWN - side, span], 2 + side)

    def w_onward(side):
        span = pl.ds(first_row + side * quarter, quarter)
        return over(side, transit.at[side], wx.at[ACROSS, span], 4 + side)

    def w_share(group):
        span = pl.ds(first_row, side_rows)
        return pltpu.make_async_remote_copy(
            src_ref=wx.at[group, span], dst_ref=wx.at[group, span],
            send_sem=w_send.at[5 + group], recv_sem=w_recv.at[5 + group],
            device_id={"seq": mate}, device_id_type=MESH,
        )

    def penalty(distance):
        other = s - distance
        same = docs[jnp.maximum(other, 0)] == docs[s]
        return jnp.where(same & (other >= 0) & (distance > 0), 0.0, FAR).astype(jnp.float32)

    def absorb(first, count, penalties):
        keys = kv[first:first + count, 0].reshape(count * BLK, HD)
        values = kv[first:first + count, 1].reshape(count * BLK, HD)
        scores = lax.dot_general(
            keys, qs[...], (((1,), (1,)), ((), ())), preferred_element_type=jnp.float32
        )
        parts = [scores[i * BLK:(i + 1) * BLK] for i in range(count)]
        old = row_max[...]
        new = old
        for part, pen in zip(parts, penalties):
            new = jnp.maximum(new, jnp.max(part, axis=0, keepdims=True) - pen)
        factor = jnp.exp2((old - new) * COEF)
        total = row_sum[...] * factor
        weights = []
        for part, pen in zip(parts, penalties):
            weight = jnp.exp2((part - (new + pen)) * COEF)
            total = total + jnp.sum(weight, axis=0, keepdims=True)
            weights.append(weight.astype(jnp.bfloat16))
        product = lax.dot_general(
            values, jnp.concatenate(weights, axis=0), (((0,), (0,)), ((), ())),
            preferred_element_type=jnp.float32,
        )
        acc[...] = acc[...] * factor + product
        row_max[...] = new
        row_sum[...] = total

    k_load.wait()
    spread(0, 0)
    v_load.wait()
    spread(0, 1)
    spread(0, WHOLE)
    share(0).start()
    for side in (0, 1):
        w_first(side).start()
    for side in (0, 1):
        w_direct(side).start()

    docs_load.wait()
    q_load.wait()
    for g in range(GROUP):
        qs[g * BLK:(g + 1) * BLK, :] = q_in[:, g * HD:(g + 1) * HD]

    scores = lax.dot_general(
        kv[0, 0], qs[...], (((1,), (1,)), ((), ())), preferred_element_type=jnp.float32
    )
    key_at = lax.broadcasted_iota(jnp.int32, (BLK, rows), 0)
    query_at = lax.rem(lax.broadcasted_iota(jnp.int32, (BLK, rows), 1), BLK)
    scores = jnp.where(key_at <= query_at, scores, -FAR)
    top = jnp.max(scores, axis=0, keepdims=True)
    weight = jnp.exp2((scores - top) * COEF)
    row_max[...] = top
    row_sum[...] = jnp.sum(weight, axis=0, keepdims=True)
    acc[...] = lax.dot_general(
        kv[0, 1], weight.astype(jnp.bfloat16), (((0,), (0,)), ((), ())),
        preferred_element_type=jnp.float32,
    )

    skew = 2 * lax.rem(s, 2) - 1

    def mine(chips):
        absorb(SLOT[chips[0]], len(chips), [penalty(2 * c) for c in chips])

    def other(chips):
        shared(*chips)
        absorb(COUNT + SLOT[chips[0]], len(chips), [penalty(2 * c + skew) for c in chips])

    arrive(*CHUNKS[0], 16)
    mine(CHUNKS[0])
    arrive(*CHUNKS[1])
    for side in (0, 1):
        w_first(side).wait_recv()
        w_onward(side).start()
    other((0, 16))
    other(CHUNKS[0])
    mine(CHUNKS[1])
    arrive(*CHUNKS[2])
    other(CHUNKS[1])
    mine(CHUNKS[2])
    other(CHUNKS[2])
    arrive(*CHUNKS[3])
    mine(CHUNKS[3])
    for side in (0, 1):
        w_direct(side).wait_recv()
        w_share(DOWN - side).start()
    other(CHUNKS[3])

    scaled = acc[...] / row_sum[...]
    for g in range(GROUP):
        att[:, g * HD:(g + 1) * HD] = scaled[:, g * BLK:(g + 1) * BLK].T.astype(jnp.bfloat16)

    def a_give(side, piece):
        span = pl.ds(piece * token_half, token_half)
        return pltpu.make_async_remote_copy(
            src_ref=att.at[span], dst_ref=ax.at[1 - side, span],
            send_sem=a_send.at[side, piece], recv_sem=a_recv.at[side, piece],
            device_id={"head": up if side == 0 else down}, device_id_type=MESH,
        )

    def a_onward(side):
        span = pl.ds(side * token_half, token_half)
        return pltpu.make_async_remote_copy(
            src_ref=ax.at[1 - side, span], dst_ref=ax.at[2, span],
            send_sem=a_send.at[side, 2], recv_sem=a_recv.at[side, 2],
            device_id={"head": up if side == 0 else down}, device_id_type=MESH,
        )

    for side, piece in ((0, 0), (1, 1), (0, 1), (1, 0)):
        a_give(side, piece).start()
    w_own.wait()
    mixed[...] = jnp.dot(att[...], wx[OWN], preferred_element_type=jnp.float32)
    for side in (0, 1):
        a_give(side, side).wait_recv()
        a_onward(side).start()
    for side in (0, 1):
        w_onward(side).wait_recv()
    w_share(ACROSS).start()
    for route in ROUTES:
        send(*route).wait_send()
    for chips in SLOTS:
        share(chips).wait_send()
    for side in (0, 1):
        w_first(side).wait_send()
        w_direct(side).wait_send()
        w_onward(side).wait_send()
        w_share(DOWN - side).wait_send()
        for piece in (0, 1):
            a_give(side, piece).wait_send()
    for side in (0, 1):
        a_give(side, 1 - side).wait_recv()
        w_share(DOWN - side).wait_recv()
        mixed[...] += jnp.dot(ax[1 - side], wx[DOWN - side], preferred_element_type=jnp.float32)
    w_share(ACROSS).wait_recv()
    for side in (0, 1):
        a_onward(side).wait_recv()
    out[...] = (
        mixed[...] + jnp.dot(ax[2], wx[ACROSS], preferred_element_type=jnp.float32)
    ).astype(jnp.bfloat16)

    w_share(ACROSS).wait_send()
    for side in (0, 1):
        a_onward(side).wait_send()


def local(query_states, key_states, value_states, out_weight, block_docs):
    query_states, key_states, value_states, out_weight, block_docs = [pltpu.with_memory_space_constraint(a, pltpu.HBM) for a in (query_states, key_states, value_states, out_weight, block_docs)]
    tokens = query_states.shape[0]
    model = out_weight.shape[1]
    width = model // lax.axis_size("head")
    rows = GROUP * BLK
    any_space = pl.BlockSpec(memory_space=pltpu.HBM)
    return pl.pallas_call(
        kernel,
        out_shape=jax.ShapeDtypeStruct((tokens, width), jnp.bfloat16),
        in_specs=[any_space] * 5,
        out_specs=pl.BlockSpec(memory_space=pltpu.VMEM),
        scratch_shapes=[
            pltpu.VMEM((tokens, rows), jnp.bfloat16),
            pltpu.VMEM((rows, HD), jnp.bfloat16),
            pltpu.VMEM((2 * COUNT, 2, BLK, HD), jnp.bfloat16),
            pltpu.VMEM((4, rows, width), jnp.bfloat16),
            pltpu.VMEM((2, rows // 4, width), jnp.bfloat16),
            pltpu.VMEM((HD, rows), jnp.float32),
            pltpu.VMEM((1, rows), jnp.float32),
            pltpu.VMEM((1, rows), jnp.float32),
            pltpu.VMEM((tokens, rows), jnp.bfloat16),
            pltpu.VMEM((3, tokens, rows), jnp.bfloat16),
            pltpu.VMEM((tokens, width), jnp.float32),
            pltpu.SMEM((128,), jnp.int32),
            pltpu.SemaphoreType.DMA((5,)),
            pltpu.SemaphoreType.DMA((len(ROUTES),)),
            pltpu.SemaphoreType.DMA((COUNT,)),
            pltpu.SemaphoreType.DMA((COUNT, 3)),
            pltpu.SemaphoreType.DMA((COUNT,)),
            pltpu.SemaphoreType.DMA((9,)),
            pltpu.SemaphoreType.DMA((9,)),
            pltpu.SemaphoreType.DMA((2, 3)),
            pltpu.SemaphoreType.DMA((2, 3)),
        ],
        compiler_params=pltpu.CompilerParams(
            collective_id=0, has_side_effects=True, vmem_limit_bytes=20 << 20
        ),
    )(block_docs, query_states, key_states, value_states, out_weight)


def solution(mesh):
    return jax.shard_map(
        local,
        mesh=mesh,
        in_specs=(P("seq", "head"), P("seq", "head"), P("seq", "head"), P("head", None), P()),
        out_specs=P("seq", "head"),
        check_vma=False,
    )
```

```python
import functools

import jax
import jax.numpy as jnp
from jax import lax
from jax.experimental import pallas as pl
from jax.experimental.pallas import tpu as pltpu
from jax.sharding import PartitionSpec as P

HD = 128
BLK = 128
GROUP = 4
CHAIN = ((0, 2), (0, 14), (2, 4), (14, 12), (4, 6), (12, 10))
LEAVES = (
    (0, 1), (0, 15), (0, 16),
    (2, 3), (14, 13), (4, 5), (12, 11), (6, 7), (10, 9),
)
LAST = ((6, 8, 0), (10, 8, 1))
SLOTS = (0, 16, 2, 14, 1, 15, 4, 12, 3, 13, 6, 10, 5, 11, 7, 9, 8)
OWN, UP, DOWN, ACROSS = range(4)
CHUNKS = ((2, 14, 1, 15), (4, 12, 3, 13), (6, 10, 5, 11), (7, 9, 8))
COUNT = len(SLOTS)
SLOT = {chips: at for at, chips in enumerate(SLOTS)}
PARTS = (0, 1)
WHOLE = 2
ROUTES = tuple((a, b, p) for a, b in CHAIN for p in PARTS) + LAST + tuple((a, b, WHOLE) for a, b in LEAVES)
PARENT = {(b, p): a for a, b, p in ROUTES}
STEPS = tuple(sorted({b - a for a, b, _ in ROUTES}))
COEF = 1.4426950408889634 / HD**0.5
FAR = 1e30
MESH = pl.DeviceIdType.MESH


def kernel(
    docs_hbm, q_hbm, k_hbm, v_hbm, w_hbm, out,
    q_in, qs, kv, wx, transit, acc, row_max, row_sum, att, ax, mixed,
    docs, loc_sem, send_sem, share_send, recv_sem, share_recv, w_send, w_recv, a_send, a_recv,
):
    s = lax.axis_index("seq")
    y = lax.axis_index("head")
    n = lax.axis_size("seq")
    heads = lax.axis_size("head")
    rows = BLK * GROUP
    width = wx.shape[2]
    side_rows = rows // 2
    quarter = rows // 4
    token_half = BLK // 2
    reach = {step: lax.rem(s + n + 2 * step, n) for step in STEPS}
    back = {step: lax.rem(s + n - 2 * step, n) for step in STEPS if -step not in STEPS}
    mate = s + 1 - 2 * lax.rem(s, 2)
    up = lax.rem(y + 1, heads)
    down = lax.rem(y + heads - 1, heads)
    across = lax.rem(y + 2, heads)

    barrier = pltpu.get_barrier_semaphore()
    for peer in (*reach.values(), *back.values(), mate):
        pl.semaphore_signal(barrier, inc=1, device_id={"seq": peer}, device_id_type=MESH)
    for peer in (up, down):
        pl.semaphore_signal(barrier, inc=1, device_id={"head": peer}, device_id_type=MESH)

    k_load = pltpu.make_async_copy(k_hbm, kv.at[0, 0], loc_sem.at[0])
    v_load = pltpu.make_async_copy(v_hbm, kv.at[0, 1], loc_sem.at[1])
    q_load = pltpu.make_async_copy(q_hbm, q_in, loc_sem.at[2])
    docs_load = pltpu.make_async_copy(docs_hbm, docs, loc_sem.at[4])
    docs_load.start()
    k_load.start()
    v_load.start()
    q_load.start()

    def columns(dest):
        return pl.ds(pl.multiple_of(dest * width, width), width)

    w_own = pltpu.make_async_copy(w_hbm.at[:, columns(y)], wx.at[OWN], loc_sem.at[3])
    w_own.start()
    pl.semaphore_wait(barrier, len(reach) + len(back) + 3)

    def view(slot, part):
        return kv.at[slot] if part == WHOLE else kv.at[slot, part]

    def send(frm, to, part):
        route = ROUTES.index((frm, to, part))
        return pltpu.make_async_remote_copy(
            src_ref=(k_hbm, v_hbm)[part] if frm == 0 and part < WHOLE else view(SLOT[frm], part),
            dst_ref=view(SLOT[to], part),
            send_sem=send_sem.at[route],
            recv_sem=recv_sem.at[SLOT[to], part],
            device_id={"seq": reach[to - frm]},
            device_id_type=MESH,
        )

    def share(chips):
        return pltpu.make_async_remote_copy(
            src_ref=kv.at[SLOT[chips]],
            dst_ref=kv.at[COUNT + SLOT[chips]],
            send_sem=share_send.at[SLOT[chips]],
            recv_sem=share_recv.at[SLOT[chips]],
            device_id={"seq": mate},
            device_id_type=MESH,
        )

    def spread(chips, part):
        for a, b, p in ROUTES:
            if (a, p) == (chips, part):
                send(a, b, p).start()

    def arrive(*chips):
        for part in PARTS:
            for c in chips:
                if (c, part) in PARENT:
                    send(PARENT[c, part], c, part).wait_recv()
                    spread(c, part)
        for c in chips:
            if (c, WHOLE) in PARENT:
                send(PARENT[c, WHOLE], c, WHOLE).wait_recv()
            spread(c, WHOLE)
            share(c).start()

    def shared(*chips):
        for c in chips:
            share(c).wait_recv()

    first_row = pl.multiple_of(lax.rem(s, 2) * side_rows, side_rows)

    def over(side, src, dst, at):
        return pltpu.make_async_remote_copy(
            src_ref=src, dst_ref=dst, send_sem=w_send.at[at], recv_sem=w_recv.at[at],
            device_id={"head": up if side == 0 else down}, device_id_type=MESH,
        )

    def w_first(side):
        span = pl.ds(first_row + side * quarter, quarter)
        return over(side, w_hbm.at[span, columns(across)], transit.at[side], side)

    def w_direct(side):
        span = pl.ds(first_row, side_rows)
        dest = up if side == 0 else down
        return over(side, w_hbm.at[span, columns(dest)], wx.at[DOWN - side, span], 2 + side)

    def w_onward(side):
        span = pl.ds(first_row + side * quarter, quarter)
        return over(side, transit.at[side], wx.at[ACROSS, span], 4 + side)

    def w_share(group):
        span = pl.ds(first_row, side_rows)
        return pltpu.make_async_remote_copy(
            src_ref=wx.at[group, span], dst_ref=wx.at[group, span],
            send_sem=w_send.at[5 + group], recv_sem=w_recv.at[5 + group],
            device_id={"seq": mate}, device_id_type=MESH,
        )

    def penalty(distance):
        other = s - distance
        same = docs[jnp.maximum(other, 0)] == docs[s]
        return jnp.where(same & (other >= 0) & (distance > 0), 0.0, FAR).astype(jnp.float32)

    def absorb(first, count, penalties):
        keys = kv[first:first + count, 0].reshape(count * BLK, HD)
        values = kv[first:first + count, 1].reshape(count * BLK, HD)
        scores = lax.dot_general(
            keys, qs[...], (((1,), (1,)), ((), ())), preferred_element_type=jnp.float32
        )
        parts = [scores[i * BLK:(i + 1) * BLK] for i in range(count)]
        old = row_max[...]
        new = old
        for part, pen in zip(parts, penalties):
            new = jnp.maximum(new, jnp.max(part, axis=0, keepdims=True) - pen)
        factor = jnp.exp2((old - new) * COEF)
        total = row_sum[...] * factor
        weights = []
        for part, pen in zip(parts, penalties):
            weight = jnp.exp2((part - (new + pen)) * COEF)
            total = total + jnp.sum(weight, axis=0, keepdims=True)
            weights.append(weight.astype(jnp.bfloat16))
        product = lax.dot_general(
            values, jnp.concatenate(weights, axis=0), (((0,), (0,)), ((), ())),
            preferred_element_type=jnp.float32,
        )
        acc[...] = acc[...] * factor + product
        row_max[...] = new
        row_sum[...] = total

    spread(0, 0)
    spread(0, 1)
    k_load.wait()
    v_load.wait()
    spread(0, WHOLE)
    share(0).start()
    for side in (0, 1):
        w_first(side).start()
    for side in (0, 1):
        w_direct(side).start()

    docs_load.wait()
    q_load.wait()
    for g in range(GROUP):
        qs[g * BLK:(g + 1) * BLK, :] = q_in[:, g * HD:(g + 1) * HD]

    scores = lax.dot_general(
        kv[0, 0], qs[...], (((1,), (1,)), ((), ())), preferred_element_type=jnp.float32
    )
    key_at = lax.broadcasted_iota(jnp.int32, (BLK, rows), 0)
    query_at = lax.rem(lax.broadcasted_iota(jnp.int32, (BLK, rows), 1), BLK)
    scores = jnp.where(key_at <= query_at, scores, -FAR)
    top = jnp.max(scores, axis=0, keepdims=True)
    weight = jnp.exp2((scores - top) * COEF)
    row_max[...] = top
    row_sum[...] = jnp.sum(weight, axis=0, keepdims=True)
    acc[...] = lax.dot_general(
        kv[0, 1], weight.astype(jnp.bfloat16), (((0,), (0,)), ((), ())),
        preferred_element_type=jnp.float32,
    )

    skew = 2 * lax.rem(s, 2) - 1

    def mine(chips):
        absorb(SLOT[chips[0]], len(chips), [penalty(2 * c) for c in chips])

    def other(chips):
        shared(*chips)
        absorb(COUNT + SLOT[chips[0]], len(chips), [penalty(2 * c + skew) for c in chips])

    arrive(*CHUNKS[0], 16)
    mine(CHUNKS[0])
    arrive(*CHUNKS[1])
    for side in (0, 1):
        w_first(side).wait_recv()
        w_onward(side).start()
    other((0, 16))
    other(CHUNKS[0])
    mine(CHUNKS[1])
    arrive(*CHUNKS[2])
    other(CHUNKS[1])
    mine(CHUNKS[2])
    other(CHUNKS[2])
    arrive(*CHUNKS[3])
    mine(CHUNKS[3])
    for side in (0, 1):
        w_direct(side).wait_recv()
        w_share(DOWN - side).start()
    other(CHUNKS[3])

    scaled = acc[...] / row_sum[...]
    for g in range(GROUP):
        att[:, g * HD:(g + 1) * HD] = scaled[:, g * BLK:(g + 1) * BLK].T.astype(jnp.bfloat16)

    def a_give(side, piece):
        span = pl.ds(piece * token_half, token_half)
        return pltpu.make_async_remote_copy(
            src_ref=att.at[span], dst_ref=ax.at[1 - side, span],
            send_sem=a_send.at[side, piece], recv_sem=a_recv.at[side, piece],
            device_id={"head": up if side == 0 else down}, device_id_type=MESH,
        )

    def a_onward(side):
        span = pl.ds(side * token_half, token_half)
        return pltpu.make_async_remote_copy(
            src_ref=ax.at[1 - side, span], dst_ref=ax.at[2, span],
            send_sem=a_send.at[side, 2], recv_sem=a_recv.at[side, 2],
            device_id={"head": up if side == 0 else down}, device_id_type=MESH,
        )

    for side, piece in ((0, 0), (1, 1), (0, 1), (1, 0)):
        a_give(side, piece).start()
    w_own.wait()
    mixed[...] = jnp.dot(att[...], wx[OWN], preferred_element_type=jnp.float32)
    for side in (0, 1):
        a_give(side, side).wait_recv()
        a_onward(side).start()
    for side in (0, 1):
        w_onward(side).wait_recv()
    w_share(ACROSS).start()
    for route in ROUTES:
        send(*route).wait_send()
    for chips in SLOTS:
        share(chips).wait_send()
    for side in (0, 1):
        w_first(side).wait_send()
        w_direct(side).wait_send()
        w_onward(side).wait_send()
        w_share(DOWN - side).wait_send()
        for piece in (0, 1):
            a_give(side, piece).wait_send()
    for side in (0, 1):
        a_give(side, 1 - side).wait_recv()
        w_share(DOWN - side).wait_recv()
        mixed[...] += jnp.dot(ax[1 - side], wx[DOWN - side], preferred_element_type=jnp.float32)
    w_share(ACROSS).wait_recv()
    for side in (0, 1):
        a_onward(side).wait_recv()
    out[...] = (
        mixed[...] + jnp.dot(ax[2], wx[ACROSS], preferred_element_type=jnp.float32)
    ).astype(jnp.bfloat16)

    w_share(ACROSS).wait_send()
    for side in (0, 1):
        a_onward(side).wait_send()


def local(query_states, key_states, value_states, out_weight, block_docs):
    query_states, key_states, value_states, out_weight, block_docs = [pltpu.with_memory_space_constraint(a, pltpu.HBM) for a in (query_states, key_states, value_states, out_weight, block_docs)]
    tokens = query_states.shape[0]
    model = out_weight.shape[1]
    width = model // lax.axis_size("head")
    rows = GROUP * BLK
    any_space = pl.BlockSpec(memory_space=pltpu.HBM)
    return pl.pallas_call(
        kernel,
        out_shape=jax.ShapeDtypeStruct((tokens, width), jnp.bfloat16),
        in_specs=[any_space] * 5,
        out_specs=pl.BlockSpec(memory_space=pltpu.VMEM),
        scratch_shapes=[
            pltpu.VMEM((tokens, rows), jnp.bfloat16),
            pltpu.VMEM((rows, HD), jnp.bfloat16),
            pltpu.VMEM((2 * COUNT, 2, BLK, HD), jnp.bfloat16),
            pltpu.VMEM((4, rows, width), jnp.bfloat16),
            pltpu.VMEM((2, rows // 4, width), jnp.bfloat16),
            pltpu.VMEM((HD, rows), jnp.float32),
            pltpu.VMEM((1, rows), jnp.float32),
            pltpu.VMEM((1, rows), jnp.float32),
            pltpu.VMEM((tokens, rows), jnp.bfloat16),
            pltpu.VMEM((3, tokens, rows), jnp.bfloat16),
            pltpu.VMEM((tokens, width), jnp.float32),
            pltpu.SMEM((128,), jnp.int32),
            pltpu.SemaphoreType.DMA((5,)),
            pltpu.SemaphoreType.DMA((len(ROUTES),)),
            pltpu.SemaphoreType.DMA((COUNT,)),
            pltpu.SemaphoreType.DMA((COUNT, 3)),
            pltpu.SemaphoreType.DMA((COUNT,)),
            pltpu.SemaphoreType.DMA((9,)),
            pltpu.SemaphoreType.DMA((9,)),
            pltpu.SemaphoreType.DMA((2, 3)),
            pltpu.SemaphoreType.DMA((2, 3)),
        ],
        compiler_params=pltpu.CompilerParams(
            collective_id=0, has_side_effects=True, vmem_limit_bytes=20 << 20
        ),
    )(block_docs, query_states, key_states, value_states, out_weight)


def solution(mesh):
    return jax.shard_map(
        local,
        mesh=mesh,
        in_specs=(P("seq", "head"), P("seq", "head"), P("seq", "head"), P("head", None), P()),
        out_specs=P("seq", "head"),
        check_vma=False,
    )
```

```python
import functools

import jax
import jax.numpy as jnp
from jax import lax
from jax.experimental import pallas as pl
from jax.experimental.pallas import tpu as pltpu
from jax.sharding import PartitionSpec as P

HD = 128
BLK = 128
GROUP = 4
CHAIN = ((0, 2), (0, 14), (2, 4), (14, 12), (4, 6), (12, 10))
LEAVES = (
    (0, 1), (0, 15), (0, 16),
    (2, 3), (14, 13), (4, 5), (12, 11), (6, 7), (10, 9),
)
LAST = ((6, 8, 0), (10, 8, 1))
SLOTS = (0, 16, 2, 14, 1, 15, 4, 12, 3, 13, 6, 10, 5, 11, 7, 9, 8)
OWN, UP, DOWN, ACROSS = range(4)
CHUNKS = ((2, 14, 1, 15), (4, 12, 3, 13), (6, 10, 5, 11), (7, 9, 8))
COUNT = len(SLOTS)
SLOT = {chips: at for at, chips in enumerate(SLOTS)}
PARTS = (0, 1)
WHOLE = 2
ROUTES = tuple((a, b, p) for a, b in CHAIN for p in PARTS) + LAST + tuple((a, b, WHOLE) for a, b in LEAVES)
PARENT = {(b, p): a for a, b, p in ROUTES}
STEPS = tuple(sorted({b - a for a, b, _ in ROUTES}))
COEF = 1.4426950408889634 / HD**0.5
FAR = 1e30
MESH = pl.DeviceIdType.MESH


def kernel(
    docs_hbm, q_hbm, k_hbm, v_hbm, w_hbm, out,
    q_in, qs, kv, wx, transit, acc, row_max, row_sum, att, ax, mixed,
    docs, loc_sem, send_sem, share_send, recv_sem, share_recv, w_send, w_recv, a_send, a_recv,
):
    s = lax.axis_index("seq")
    y = lax.axis_index("head")
    n = lax.axis_size("seq")
    heads = lax.axis_size("head")
    rows = BLK * GROUP
    width = wx.shape[2]
    side_rows = rows // 2
    quarter = rows // 4
    token_half = BLK // 2
    token_part = BLK // 4
    reach = {step: lax.rem(s + n + 2 * step, n) for step in STEPS}
    back = {step: lax.rem(s + n - 2 * step, n) for step in STEPS if -step not in STEPS}
    mate = s + 1 - 2 * lax.rem(s, 2)
    up = lax.rem(y + 1, heads)
    down = lax.rem(y + heads - 1, heads)
    across = lax.rem(y + 2, heads)

    k_load = pltpu.make_async_copy(k_hbm, kv.at[0, 0], loc_sem.at[0])
    v_load = pltpu.make_async_copy(v_hbm, kv.at[0, 1], loc_sem.at[1])
    q_load = pltpu.make_async_copy(q_hbm, q_in, loc_sem.at[2])
    docs_load = pltpu.make_async_copy(docs_hbm, docs, loc_sem.at[4])
    docs_load.start()
    k_load.start()
    v_load.start()
    q_load.start()

    barrier = pltpu.get_barrier_semaphore()
    for peer in (*reach.values(), *back.values(), mate):
        pl.semaphore_signal(barrier, inc=1, device_id={"seq": peer}, device_id_type=MESH)
    for peer in (up, down):
        pl.semaphore_signal(barrier, inc=1, device_id={"head": peer}, device_id_type=MESH)

    def columns(dest):
        return pl.ds(pl.multiple_of(dest * width, width), width)

    w_own = pltpu.make_async_copy(w_hbm.at[:, columns(y)], wx.at[OWN], loc_sem.at[3])
    w_own.start()
    pl.semaphore_wait(barrier, len(reach) + len(back) + 3)

    def view(slot, part):
        return kv.at[slot] if part == WHOLE else kv.at[slot, part]

    def send(frm, to, part):
        route = ROUTES.index((frm, to, part))
        return pltpu.make_async_remote_copy(
            src_ref=view(SLOT[frm], part),
            dst_ref=view(SLOT[to], part),
            send_sem=send_sem.at[route],
            recv_sem=recv_sem.at[SLOT[to], part],
            device_id={"seq": reach[to - frm]},
            device_id_type=MESH,
        )

    def share(chips):
        return pltpu.make_async_remote_copy(
            src_ref=kv.at[SLOT[chips]],
            dst_ref=kv.at[COUNT + SLOT[chips]],
            send_sem=share_send.at[SLOT[chips]],
            recv_sem=share_recv.at[SLOT[chips]],
            device_id={"seq": mate},
            device_id_type=MESH,
        )

    def spread(chips, part):
        for a, b, p in ROUTES:
            if (a, p) == (chips, part):
                send(a, b, p).start()

    def arrive(*chips):
        for part in PARTS:
            for c in chips:
                if (c, part) in PARENT:
                    send(PARENT[c, part], c, part).wait_recv()
                    spread(c, part)
        for c in chips:
            if (c, WHOLE) in PARENT:
                send(PARENT[c, WHOLE], c, WHOLE).wait_recv()
            spread(c, WHOLE)
            share(c).start()

    def shared(*chips):
        for c in chips:
            share(c).wait_recv()

    first_row = pl.multiple_of(lax.rem(s, 2) * side_rows, side_rows)

    def over(side, src, dst, at):
        return pltpu.make_async_remote_copy(
            src_ref=src, dst_ref=dst, send_sem=w_send.at[at], recv_sem=w_recv.at[at],
            device_id={"head": up if side == 0 else down}, device_id_type=MESH,
        )

    def w_first(side):
        span = pl.ds(first_row + side * quarter, quarter)
        return over(side, w_hbm.at[span, columns(across)], transit.at[side], side)

    def w_direct(side):
        span = pl.ds(first_row, side_rows)
        dest = up if side == 0 else down
        return over(side, w_hbm.at[span, columns(dest)], wx.at[DOWN - side, span], 2 + side)

    def w_onward(side):
        span = pl.ds(first_row + side * quarter, quarter)
        return over(side, transit.at[side], wx.at[ACROSS, span], 4 + side)

    def w_share(group):
        span = pl.ds(first_row, side_rows)
        return pltpu.make_async_remote_copy(
            src_ref=wx.at[group, span], dst_ref=wx.at[group, span],
            send_sem=w_send.at[5 + group], recv_sem=w_recv.at[5 + group],
            device_id={"seq": mate}, device_id_type=MESH,
        )

    def penalty(distance):
        other = s - distance
        same = docs[jnp.maximum(other, 0)] == docs[s]
        return jnp.where(same & (other >= 0) & (distance > 0), 0.0, FAR).astype(jnp.float32)

    def absorb(first, count, penalties):
        keys = kv[first:first + count, 0].reshape(count * BLK, HD)
        values = kv[first:first + count, 1].reshape(count * BLK, HD)
        scores = lax.dot_general(
            keys, qs[...], (((1,), (1,)), ((), ())), preferred_element_type=jnp.float32
        )
        parts = [scores[i * BLK:(i + 1) * BLK] for i in range(count)]
        old = row_max[...]
        new = old
        for part, pen in zip(parts, penalties):
            new = jnp.maximum(new, jnp.max(part, axis=0, keepdims=True) - pen)
        factor = jnp.exp2((old - new) * COEF)
        total = row_sum[...] * factor
        weights = []
        for part, pen in zip(parts, penalties):
            weight = jnp.exp2((part - (new + pen)) * COEF)
            total = total + jnp.sum(weight, axis=0, keepdims=True)
            weights.append(weight.astype(jnp.bfloat16))
        product = lax.dot_general(
            values, jnp.concatenate(weights, axis=0), (((0,), (0,)), ((), ())),
            preferred_element_type=jnp.float32,
        )
        acc[...] = acc[...] * factor + product
        row_max[...] = new
        row_sum[...] = total

    k_load.wait()
    spread(0, 0)
    v_load.wait()
    spread(0, 1)
    spread(0, WHOLE)
    share(0).start()
    for side in (0, 1):
        w_first(side).start()
    for side in (0, 1):
        w_direct(side).start()

    docs_load.wait()
    q_load.wait()
    for g in range(GROUP):
        qs[g * BLK:(g + 1) * BLK, :] = q_in[:, g * HD:(g + 1) * HD]

    scores = lax.dot_general(
        kv[0, 0], qs[...], (((1,), (1,)), ((), ())), preferred_element_type=jnp.float32
    )
    key_at = lax.broadcasted_iota(jnp.int32, (BLK, rows), 0)
    query_at = lax.rem(lax.broadcasted_iota(jnp.int32, (BLK, rows), 1), BLK)
    scores = jnp.where(key_at <= query_at, scores, -FAR)
    top = jnp.max(scores, axis=0, keepdims=True)
    weight = jnp.exp2((scores - top) * COEF)
    row_max[...] = top
    row_sum[...] = jnp.sum(weight, axis=0, keepdims=True)
    acc[...] = lax.dot_general(
        kv[0, 1], weight.astype(jnp.bfloat16), (((0,), (0,)), ((), ())),
        preferred_element_type=jnp.float32,
    )

    skew = 2 * lax.rem(s, 2) - 1

    def mine(chips):
        absorb(SLOT[chips[0]], len(chips), [penalty(2 * c) for c in chips])

    def other(chips):
        shared(*chips)
        absorb(COUNT + SLOT[chips[0]], len(chips), [penalty(2 * c + skew) for c in chips])

    arrive(*CHUNKS[0], 16)
    mine(CHUNKS[0])
    arrive(*CHUNKS[1])
    for side in (0, 1):
        w_first(side).wait_recv()
        w_onward(side).start()
    other((0, 16))
    other(CHUNKS[0])
    mine(CHUNKS[1])
    arrive(*CHUNKS[2])
    other(CHUNKS[1])
    mine(CHUNKS[2])
    other(CHUNKS[2])
    arrive(*CHUNKS[3])
    mine(CHUNKS[3])
    for side in (0, 1):
        w_direct(side).wait_recv()
        w_share(DOWN - side).start()
    other(CHUNKS[3])

    scaled = acc[...] / row_sum[...]
    for g in range(GROUP):
        att[:, g * HD:(g + 1) * HD] = scaled[:, g * BLK:(g + 1) * BLK].T.astype(jnp.bfloat16)

    def a_give(side, piece):
        span = pl.ds(piece * token_part, token_part)
        return pltpu.make_async_remote_copy(
            src_ref=att.at[span], dst_ref=ax.at[1 - side, span],
            send_sem=a_send.at[side, piece], recv_sem=a_recv.at[side, piece],
            device_id={"head": up if side == 0 else down}, device_id_type=MESH,
        )

    def a_onward(side, piece):
        span = pl.ds((2 * side + piece) * token_part, token_part)
        return pltpu.make_async_remote_copy(
            src_ref=ax.at[1 - side, span], dst_ref=ax.at[2, span],
            send_sem=a_send.at[side, 4 + piece], recv_sem=a_recv.at[side, 4 + piece],
            device_id={"head": up if side == 0 else down}, device_id_type=MESH,
        )

    for piece in (0, 1):
        for side in (0, 1):
            a_give(side, 2 * side + piece).start()
    for piece in (0, 1):
        for side in (0, 1):
            a_give(side, 2 - 2 * side + piece).start()
    w_own.wait()
    mixed[...] = jnp.dot(att[...], wx[OWN], preferred_element_type=jnp.float32)
    for piece in (0, 1):
        for side in (0, 1):
            a_give(side, 2 * side + piece).wait_recv()
            a_onward(side, piece).start()
    for side in (0, 1):
        w_onward(side).wait_recv()
    w_share(ACROSS).start()
    for route in ROUTES:
        send(*route).wait_send()
    for chips in SLOTS:
        share(chips).wait_send()
    for side in (0, 1):
        w_first(side).wait_send()
        w_direct(side).wait_send()
        w_onward(side).wait_send()
        w_share(DOWN - side).wait_send()
        for piece in range(4):
            a_give(side, piece).wait_send()
    for side in (0, 1):
        for piece in (0, 1):
            a_give(side, 2 - 2 * side + piece).wait_recv()
        w_share(DOWN - side).wait_recv()
        mixed[...] += jnp.dot(ax[1 - side], wx[DOWN - side], preferred_element_type=jnp.float32)
    w_share(ACROSS).wait_recv()
    for side in (0, 1):
        for piece in (0, 1):
            a_onward(side, piece).wait_recv()
    out[...] = (
        mixed[...] + jnp.dot(ax[2], wx[ACROSS], preferred_element_type=jnp.float32)
    ).astype(jnp.bfloat16)

    w_share(ACROSS).wait_send()
    for side in (0, 1):
        for piece in (0, 1):
            a_onward(side, piece).wait_send()


def local(query_states, key_states, value_states, out_weight, block_docs):
    query_states, key_states, value_states, out_weight, block_docs = [pltpu.with_memory_space_constraint(a, pltpu.HBM) for a in (query_states, key_states, value_states, out_weight, block_docs)]
    tokens = query_states.shape[0]
    model = out_weight.shape[1]
    width = model // lax.axis_size("head")
    rows = GROUP * BLK
    any_space = pl.BlockSpec(memory_space=pltpu.HBM)
    return pl.pallas_call(
        kernel,
        out_shape=jax.ShapeDtypeStruct((tokens, width), jnp.bfloat16),
        in_specs=[any_space] * 5,
        out_specs=pl.BlockSpec(memory_space=pltpu.VMEM),
        scratch_shapes=[
            pltpu.VMEM((tokens, rows), jnp.bfloat16),
            pltpu.VMEM((rows, HD), jnp.bfloat16),
            pltpu.VMEM((2 * COUNT, 2, BLK, HD), jnp.bfloat16),
            pltpu.VMEM((4, rows, width), jnp.bfloat16),
            pltpu.VMEM((2, rows // 4, width), jnp.bfloat16),
            pltpu.VMEM((HD, rows), jnp.float32),
            pltpu.VMEM((1, rows), jnp.float32),
            pltpu.VMEM((1, rows), jnp.float32),
            pltpu.VMEM((tokens, rows), jnp.bfloat16),
            pltpu.VMEM((3, tokens, rows), jnp.bfloat16),
            pltpu.VMEM((tokens, width), jnp.float32),
            pltpu.SMEM((128,), jnp.int32),
            pltpu.SemaphoreType.DMA((5,)),
            pltpu.SemaphoreType.DMA((len(ROUTES),)),
            pltpu.SemaphoreType.DMA((COUNT,)),
            pltpu.SemaphoreType.DMA((COUNT, 3)),
            pltpu.SemaphoreType.DMA((COUNT,)),
            pltpu.SemaphoreType.DMA((9,)),
            pltpu.SemaphoreType.DMA((9,)),
            pltpu.SemaphoreType.DMA((2, 6)),
            pltpu.SemaphoreType.DMA((2, 6)),
        ],
        compiler_params=pltpu.CompilerParams(
            collective_id=0, has_side_effects=True, vmem_limit_bytes=20 << 20
        ),
    )(block_docs, query_states, key_states, value_states, out_weight)


def solution(mesh):
    return jax.shard_map(
        local,
        mesh=mesh,
        in_specs=(P("seq", "head"), P("seq", "head"), P("seq", "head"), P("head", None), P()),
        out_specs=P("seq", "head"),
        check_vma=False,
    )
```
